32 devices in a mesh: frame: 8 (over y, x, core), pix: 4 (over z).
Axes of the slice: x: 2, y: 2, z: 4, core: 2. Of those that a mesh axis runs over, the one named last changes fastest.
Arguments:
- frames: float32 [2048, 1024], P('frame', 'pix'), may hold values from 0.1 to 10
- roi_ids: int32 [1024, 1], P('pix'), may hold values from 0 to 3; in each aligned block of 256 rows (0 to 255, 256 to 511, ...) at most 96 rows name the same one
- roi_order: int32 [4], replicated, may hold values from 0 to 3, each once
Outputs:
- correlation: float32 [4, 2048, 2048], P('pix', 'frame')
The draws below stay inside these ranges and needn't reach their ends.
Inputs may be any that keep to these rules, and one draw needn't show every extreme that they name: `roi_ids`: among the 256 pixels of one pix index no q-ROI has more than 96 pixels, and some q-ROI has exactly 96; every q-ROI has at least one pixel. `roi_order`: each q-ROI appears once; owner slot j lies on pix index j.
All inputs are finite; a program needn't handle non-finite values.
Results may differ from the reference program's by a relative error of at most 0.0003.
Values sent between devices are 32-bit elements; how exact they have to be, the bound alone decides.
A program may use at most 64 MiB of HBM per device.

```python
import math
import jax
import jax.numpy as jnp
import numpy as np
from jax import lax

SLOT = 96
ROIS = 4
PIX_DEV = 256
PIXELS = 1024
FRAMES = 2048
CAP = 384


def block_scale(stream_key, shape, cuts, least, high):
    level = 1.0
    for dim, parts in cuts:
        draws = jax.random.uniform(jax.random.fold_in(jax.random.fold_in(stream_key, 6), dim), (parts,), jnp.float32, least / len(cuts), high / len(cuts))
        level = level * jnp.repeat(jnp.exp(draws), shape[dim] // parts).reshape((-1,) + (1,) * (len(shape) - 1 - dim))
    return level


def assign_block(rng, own, number, rows, number_of, top, bound, skew):
    sequence = jax.random.permutation(rng, number_of)
    heavy_load, ordinary = shares(number_of, rows * top, bound, skew, True), shares(number_of, rows * top, bound, skew, False)
    places = jnp.arange(number_of)

    def named(lengths, turn):
        used = int((lengths > 0).sum())
        fixed = max(1, used // 4)
        moved = fixed + (places - fixed + turn * (used - fixed)) % max(1, number_of - fixed)
        return jnp.zeros((number_of,), jnp.int32).at[sequence[jnp.where(places < fixed, places, moved)]].set(jnp.asarray(lengths, jnp.int32))

    lengths = jnp.where(number % 4 == 0, named(heavy_load, number // 4), named(ordinary, number - number // 4 - 1))
    mixed = jax.random.permutation(jax.random.fold_in(own, 3), number_of)
    giver, taker = mixed[0:number_of // 2 * 2:2], mixed[1:number_of // 2 * 2:2]
    margin = jnp.minimum(lengths[giver] - 1, bound - lengths[taker]) // 2
    margin = jnp.where((giver == sequence[0]) | (taker == sequence[0]) | (lengths[taker] == 0), 0, jnp.maximum(margin, 0))
    moved = jax.random.randint(jax.random.fold_in(own, 4), (number_of // 2,), 0, 1 << 20) % (margin + 1)
    lengths = lengths.at[giver].add(-moved).at[taker].add(moved)
    members = jnp.searchsorted(jnp.cumsum(lengths), jnp.arange(rows * top), side="right").astype(jnp.int32)
    grid = members.reshape(top, rows).T
    grid = grid[jax.random.permutation(jax.random.fold_in(own, 1), rows)]
    turn = jax.random.randint(jax.random.fold_in(own, 2), (rows, 1), 0, top)
    return jnp.take_along_axis(grid, (jnp.arange(top)[None, :] + turn) % top, axis=1)


def shares(count, total, reach, lean, full):
    weights = [(1 << 20) // math.isqrt(grade ** lean) + 1 for grade in range(1, count + 1)]
    largest = reach if full else min(reach, max(-(-total // count), total * weights[0] // sum(weights)))
    least = 1 if total - largest >= count - 1 else 0
    counts, surplus = [largest] + [least] * (count - 1), total - largest - least * (count - 1)
    while surplus > 0:
        candidates = [i for i in range(1, count) if counts[i] < largest] or [i for i in range(1, count) if counts[i] < reach]
        pool, budget = sum([weights[i] for i in candidates]), surplus
        for i in candidates:
            extra = min(reach - counts[i], max(1, budget * weights[i] // pool), surplus)
            counts[i] = counts[i] + extra
            surplus = surplus - extra
    return np.array(counts)


def setup_inputs(seed: int = 0) -> dict:
    streams_of = jax.random.split(jax.random.key(seed), 4)
    frames = jnp.clip(jnp.exp(math.log(10.0) - 4.6051702 * jax.random.uniform(streams_of[0], (FRAMES, PIXELS), jnp.float32) ** block_scale(streams_of[0], (FRAMES, PIXELS), ((0, 8), (1, 4)), -0.2, 0.2)), 0.1, 10.0)
    roi_ids_keys = jax.random.split(jax.random.fold_in(streams_of[1], 1), PIXELS // PIX_DEV)
    roi_ids_turns = jax.random.permutation(jax.random.fold_in(streams_of[1], 3), PIXELS // PIX_DEV)
    roi_ids = jax.vmap(lambda own, number: assign_block(jax.random.fold_in(streams_of[1], 2), own, number, PIX_DEV, ROIS, 1, SLOT, 2))(roi_ids_keys, roi_ids_turns).reshape((PIXELS, 1))
    roi_order = jax.random.permutation(streams_of[2], ROIS).astype(jnp.int32)
    return dict(frames=frames, roi_ids=roi_ids, roi_order=roi_order)


def reference(frames, roi_ids, roi_order):
    ids = roi_ids[:, 0]
    order = jnp.argsort(ids, stable=True).astype(jnp.int32)
    sorted_frames = frames[:, order]
    padded = jnp.concatenate([sorted_frames, jnp.zeros((FRAMES, CAP), jnp.float32)], axis=1)
    count = jnp.sum((ids[:, None] == jnp.arange(ROIS, dtype=jnp.int32)[None, :]).astype(jnp.int32), axis=0)
    starts = (jnp.cumsum(count) - count).astype(jnp.int32)

    def one_slot(index):
        region = roi_order[index]
        start = starts[region].astype(jnp.int32)
        columns = lax.dynamic_slice(padded, (jnp.int32(0), start), (FRAMES, CAP))
        keep = (jnp.arange(CAP, dtype=jnp.int32) < count[region]).astype(jnp.float32)
        block = columns * keep[None, :]
        gram = jnp.dot(block, block.T, precision=lax.Precision.HIGHEST, preferred_element_type=jnp.float32)
        sums = jnp.sum(block, axis=1)
        total = count[region].astype(jnp.float32)
        return total * gram / (sums[:, None] * sums[None, :])

    return lax.map(one_slot, jnp.arange(ROIS, dtype=jnp.int32))
```

```python
import functools

import jax
import jax.numpy as jnp
from jax import lax
from jax.experimental import pallas as pl
from jax.experimental.pallas import tpu as pltpu
from jax.sharding import PartitionSpec as P

SLOT = 96
MESH = pl.DeviceIdType.MESH
F32 = jnp.float32
BF16 = jnp.bfloat16


def flip(value, mask):
    bit = 1
    out = value
    while bit <= mask:
        if mask & bit:
            out = out + bit - 2 * bit * ((value // bit) % 2)
        bit *= 2
    return out


def halves(value):
    high = value.astype(BF16)
    return high, (value - high.astype(F32)).astype(BF16)


def kernel(npix, order_ref, ids_ref, frames_ref, out_ref, packed, grid, lhs, cols, sems_send, sems_recv):
    frame = lax.axis_index("frame")
    pix = lax.axis_index("pix")
    fr, npx = frames_ref.shape
    slot = SLOT
    half = slot // 2

    def at_frame(mask):
        return (flip(frame, mask), pix)

    def at_pix(mask):
        return (frame, flip(pix, mask))

    peers = [at_frame(1), at_frame(2), at_frame(4)] + [at_pix(k) for k in range(1, npix)]
    barrier = pltpu.get_barrier_semaphore()
    for peer in peers:
        pl.semaphore_signal(barrier, inc=1, device_id=peer, device_id_type=MESH)

    below = lax.broadcasted_iota(jnp.int32, (npx, npx), 0)
    across = lax.broadcasted_iota(jnp.int32, (npx, npx), 1)
    column = jnp.broadcast_to(ids_ref[...], (npx, npx))
    row = jnp.sum(jnp.where(below == across, column, 0), axis=0, keepdims=True)
    earlier = jnp.logical_and(column == row, below < across)
    rank = jnp.sum(earlier.astype(jnp.int32), axis=0, keepdims=True)
    place = lax.broadcasted_iota(jnp.int32, (slot, npx), 0)
    picks = []
    for k in range(npix):
        region = order_ref[flip(pix, k)]
        wanted = jnp.where(row == region, rank, -1)
        picks.append((wanted == place).astype(F32).astype(BF16))
    pick = jnp.concatenate(picks, axis=0)
    rest = frames_ref[...]
    total = None
    for _ in range(3):
        piece = rest.astype(BF16)
        rest = rest - piece.astype(F32)
        part = lax.dot_general(pick, piece, (((1,), (1,)), ((), ())), preferred_element_type=F32)
        total = part if total is None else total + part
    for k in range(1, npix):
        packed[k - 1] = total[k * slot:(k + 1) * slot]
    grid[0, 0] = total[:slot]

    pl.semaphore_wait(barrier, len(peers))

    copies = []

    def send(source, target, peer):
        number = len(copies)
        copy = pltpu.make_async_remote_copy(
            src_ref=source,
            dst_ref=target,
            send_sem=sems_send.at[number],
            recv_sem=sems_recv.at[number],
            device_id=peer,
            device_id_type=MESH,
        )
        copy.start()
        copies.append(copy)
        return copy

    low, high = pl.ds(0, half), pl.ds(half, half)
    arrive = {}

    def spread(k):
        arrive["x", k] = send(grid.at[0, k], grid.at[2, k], at_frame(2))
        arrive["y", k] = send(grid.at[0, k], grid.at[4, k], at_frame(4))
        arrive[1, k] = send(grid.at[0, k], grid.at[1, k], at_frame(1))

    def relay(k):
        arrive["x", k].wait_recv()
        arrive["low", k] = send(grid.at[2, k, low], grid.at[6, k, low], at_frame(4))
        arrive[3, k] = send(grid.at[2, k], grid.at[3, k], at_frame(1))
        arrive["y", k].wait_recv()
        arrive["high", k] = send(grid.at[4, k, high], grid.at[6, k, high], at_frame(2))
        arrive[5, k] = send(grid.at[4, k], grid.at[5, k], at_frame(1))

    def corner(k):
        arrive["low", k].wait_recv()
        arrive["high", k].wait_recv()
        arrive[7, k] = send(grid.at[6, k], grid.at[7, k], at_frame(1))

    state = {"sum": None, "count": None}

    def own(k):
        value = jnp.transpose(grid[0, k])
        sums = jnp.sum(value, axis=1, keepdims=True)
        count = jnp.sum((value > 0).astype(F32), axis=1, keepdims=True)
        state["sum"] = sums if k == 0 else state["sum"] + sums
        state["count"] = count if k == 0 else state["count"] + count
        top, bottom = halves(value)
        lhs[k] = jnp.concatenate([top, bottom, top], axis=1)

    def tile(r, k):
        value = grid[r, k]
        sums = jnp.sum(value, axis=0, keepdims=True)
        top, bottom = halves(value)
        rhs = jnp.concatenate([top, top, bottom], axis=0)
        part = jnp.dot(lhs[k], rhs, preferred_element_type=F32)
        where = pl.ds(pl.multiple_of(flip(frame, r) * fr, fr), fr)
        if k > 0:
            part = out_ref[0, :, where] + part
            sums = cols[r] + sums
        if k == npix - 1:
            part = part * state["row"] * (1.0 / sums)
        else:
            cols[r] = sums
        out_ref[0, :, where] = part

    def tiles(k, near):
        if near:
            own(k)
            if k == npix - 1:
                state["row"] = state["count"] / state["sum"]
            arrive[1, k].wait_recv()
            rels = (0, 1, 2, 4)
        else:
            for r in (3, 5, 7):
                arrive[r, k].wait_recv()
            rels = (6, 3, 5, 7)
        for r in rels:
            tile(r, k)

    incoming = {k: send(packed.at[k - 1], grid.at[0, k], at_pix(k)) for k in range(1, npix)}
    spread(0)
    for k in range(npix):
        if k + 1 < npix:
            incoming[k + 1].wait_recv()
            spread(k + 1)
        relay(k)
        if k > 0:
            corner(k - 1)
            tiles(k - 1, False)
        tiles(k, True)
    corner(npix - 1)
    tiles(npix - 1, False)
    for copy in copies:
        copy.wait_send()


def fused(npix, frames, roi_ids, roi_order):
    fr, npx = frames.shape
    slot = SLOT
    count = (npix - 1) + 9 * npix
    vmem = pl.BlockSpec(memory_space=pltpu.VMEM)
    return pl.pallas_call(
        functools.partial(kernel, npix),
        out_shape=jax.ShapeDtypeStruct((1, fr, 8 * fr), F32),
        in_specs=[pl.BlockSpec(memory_space=pltpu.SMEM), vmem, vmem],
        out_specs=vmem,
        scratch_shapes=[
            pltpu.VMEM((npix - 1, slot, fr), F32),
            pltpu.VMEM((8, npix, slot, fr), F32),
            pltpu.VMEM((npix, fr, 3 * slot), BF16),
            pltpu.VMEM((8, 1, fr), F32),
            pltpu.SemaphoreType.DMA((count,)),
            pltpu.SemaphoreType.DMA((count,)),
        ],
        compiler_params=pltpu.CompilerParams(
            collective_id=0, has_side_effects=True, vmem_limit_bytes=40 * 1024 * 1024
        ),
    )(roi_order, roi_ids, frames)


def shifted(value, axis, steps):
    count = lax.axis_size(axis)
    pairs = [(source, (source + steps) % count) for source in range(count)]
    return lax.ppermute(value, axis, pairs)


def per_device(frames, roi_ids, roi_order):
    fr_dev, pix_dev = frames.shape
    npix = lax.axis_size("pix")
    nframe = lax.axis_size("frame")
    rois = roi_order.shape[0]
    roi_dev = rois // npix
    slot = SLOT
    ids = roi_ids[:, 0]
    labels = jnp.arange(rois, dtype=jnp.int32)
    onehot = (ids[:, None] == labels[None, :]).astype(jnp.int32)
    rank = jnp.sum(onehot * (jnp.cumsum(onehot, axis=0) - 1), axis=1)
    holder = (roi_order[None, :] == labels[:, None]).astype(jnp.int32)
    position = jnp.sum(holder * labels[None, :], axis=1)
    target = jnp.sum(onehot * position[None, :], axis=1) * slot + rank
    buffer = jnp.zeros((rois * slot, fr_dev), jnp.float32).at[target].set(frames.T)
    buffer = buffer.reshape(npix, roi_dev, slot, fr_dev)
    local_counts = jnp.sum(onehot, axis=0)
    slot_counts = (
        jnp.sum(holder * local_counts[:, None], axis=0).astype(jnp.float32).reshape(npix, roi_dev)
    )
    own, arrived_counts = (
        lax.all_to_all(buffer, "pix", split_axis=0, concat_axis=0, tiled=True),
        lax.all_to_all(slot_counts, "pix", split_axis=0, concat_axis=0, tiled=True),
    )
    total = jnp.sum(arrived_counts, axis=0)
    own_sums = jnp.sum(own, axis=(0, 2))
    me = lax.axis_index("frame")
    width = fr_dev * nframe

    def make_tile(block):
        gram = jnp.einsum(
            "skpa,skpb->kab",
            own,
            block,
            precision=lax.Precision.HIGHEST,
            preferred_element_type=jnp.float32,
        )
        other = jnp.sum(block, axis=(0, 2))
        return total[:, None, None] * gram / (own_sums[:, :, None] * other[:, None, :])

    def place(result, block, start):
        tile = make_tile(block)
        return lax.dynamic_update_slice(result, tile, (jnp.int32(0), jnp.int32(0), start))

    result = jnp.zeros((roi_dev, fr_dev, width), jnp.float32)
    result = place(result, own, me * fr_dev)

    def turn(step, carry):
        moving, partial_out = carry
        moving = shifted(moving, "frame", 1)
        column = (me - step) % nframe
        return (moving, place(partial_out, moving, column * fr_dev))

    moving, result = lax.fori_loop(1, nframe, turn, (own, result))
    return result


def solution(mesh):
    npix, nframe = mesh.shape["pix"], mesh.shape["frame"]
    placed = (P("frame", "pix"), P("pix", None), P())

    def body(frames, roi_ids, roi_order):
        paired = nframe == 8 and npix & (npix - 1) == 0 and roi_order.shape[0] == npix
        if paired:
            return fused(npix, frames, roi_ids, roi_order)
        return per_device(frames, roi_ids, roi_order)

    return jax.shard_map(
        body, mesh=mesh, in_specs=placed, out_specs=P("pix", "frame", None), check_vma=False
    )
```

```python
import functools

import jax
import jax.numpy as jnp
from jax import lax
from jax.experimental import pallas as pl
from jax.experimental.pallas import tpu as pltpu
from jax.sharding import PartitionSpec as P

SLOT = 96
PIECES = 2
LEAD = 2
LAG = 2
WHOLE = 0
MESH = pl.DeviceIdType.MESH
F32 = jnp.float32
BF16 = jnp.bfloat16


def flip(value, mask):
    bit = 1
    out = value
    while bit <= mask:
        if mask & bit:
            out = out + bit - 2 * bit * ((value // bit) % 2)
        bit *= 2
    return out


def halves(value):
    high = value.astype(BF16)
    return high, (value - high.astype(F32)).astype(BF16)


def kernel(
    npix, order_hbm, ids_hbm, frames_hbm, out_ref, order_ref, ids_ref, frames_ref, packed, grid, lhs, cols,
    sems_load, sems_send, sems_recv
):
    frame = lax.axis_index("frame")
    pix = lax.axis_index("pix")
    fr, npx = frames_ref.shape
    loads = [
        pltpu.make_async_copy(source, target, sems_load.at[number])
        for number, (source, target) in enumerate(
            ((ids_hbm, ids_ref), (order_hbm, order_ref), (frames_hbm, frames_ref))
        )
    ]
    for load in loads:
        load.start()
    slot = SLOT
    step = slot // PIECES
    half = step // 2

    def at_frame(mask):
        return (flip(frame, mask), pix)

    def at_pix(mask):
        return (frame, flip(pix, mask))

    peers = [at_frame(1), at_frame(2), at_frame(4)] + [at_pix(k) for k in range(1, npix)]
    barrier = pltpu.get_barrier_semaphore()
    for peer in peers:
        pl.semaphore_signal(barrier, inc=1, device_id=peer, device_id_type=MESH)

    below = lax.broadcasted_iota(jnp.int32, (npx, npx), 0)
    across = lax.broadcasted_iota(jnp.int32, (npx, npx), 1)
    loads[0].wait()
    row = ids_ref[...]
    column = jnp.sum(jnp.where(below == across, row, 0), axis=1, keepdims=True)
    earlier = jnp.logical_and(column == row, below < across)
    rank = jnp.sum(earlier.astype(jnp.int32), axis=0, keepdims=True)
    place = lax.broadcasted_iota(jnp.int32, (slot, npx), 0)
    picks = []
    loads[1].wait()
    for k in range(npix):
        region = order_ref[flip(pix, k)]
        wanted = jnp.where(row == region, rank, -1)
        picks.append((wanted == place).astype(F32).astype(BF16))
    pick = jnp.concatenate(picks, axis=0)
    loads[2].wait()
    rest = frames_ref[...]
    total = None
    for _ in range(3):
        piece = rest.astype(BF16)
        rest = rest - piece.astype(F32)
        part = lax.dot_general(pick, piece, (((1,), (1,)), ((), ())), preferred_element_type=F32)
        total = part if total is None else total + part
    for k in range(1, npix):
        packed[k - 1] = total[k * slot:(k + 1) * slot]
    grid[0, 0] = total[:slot]

    pl.semaphore_wait(barrier, len(peers))

    copies = []

    def send(source, target, peer):
        number = len(copies)
        copy = pltpu.make_async_remote_copy(
            src_ref=source,
            dst_ref=target,
            send_sem=sems_send.at[number],
            recv_sem=sems_recv.at[number],
            device_id=peer,
            device_id_type=MESH,
        )
        copy.start()
        copies.append(copy)
        return copy

    arrive = {}

    def rows(piece):
        return pl.ds(piece * step, step)

    def spread(k, piece):
        part = rows(piece)
        arrive["x", k, piece] = send(grid.at[0, k, part], grid.at[2, k, part], at_frame(2))
        arrive["y", k, piece] = send(grid.at[0, k, part], grid.at[4, k, part], at_frame(4))
        arrive[1, k, piece] = send(grid.at[0, k, part], grid.at[1, k, part], at_frame(1))

    def relay(k, piece):
        part = rows(piece)
        number = k * PIECES + piece
        low, high = pl.ds(piece * step, half), pl.ds(piece * step + half, half)
        if number < WHOLE:
            low, high = (part, None) if number % 2 == 0 else (None, part)
        arrive["x", k, piece].wait_recv()
        if low is not None:
            arrive["low", k, piece] = send(grid.at[2, k, low], grid.at[6, k, low], at_frame(4))
        arrive[3, k, piece] = send(grid.at[2, k, part], grid.at[3, k, part], at_frame(1))
        arrive["y", k, piece].wait_recv()
        if high is not None:
            arrive["high", k, piece] = send(grid.at[4, k, high], grid.at[6, k, high], at_frame(2))
        arrive[5, k, piece] = send(grid.at[4, k, part], grid.at[5, k, part], at_frame(1))

    def corner(k, piece):
        for way in ("low", "high"):
            if (way, k, piece) in arrive:
                arrive[way, k, piece].wait_recv()
        part = rows(piece)
        arrive[7, k, piece] = send(grid.at[6, k, part], grid.at[7, k, part], at_frame(1))

    def landed(r, k):
        for piece in range(PIECES):
            arrive[r, k, piece].wait_recv()

    state = {"sum": None, "count": None}

    def own(k):
        value = jnp.transpose(grid[0, k])
        sums = jnp.sum(value, axis=1, keepdims=True)
        count = jnp.sum((value > 0).astype(F32), axis=1, keepdims=True)
        state["sum"] = sums if k == 0 else state["sum"] + sums
        state["count"] = count if k == 0 else state["count"] + count
        top, bottom = halves(value)
        lhs[k] = jnp.concatenate([top, bottom, top], axis=1)

    def tile(r, k):
        value = grid[r, k]
        sums = jnp.sum(value, axis=0, keepdims=True)
        top, bottom = halves(value)
        rhs = jnp.concatenate([top, top, bottom], axis=0)
        part = jnp.dot(lhs[k], rhs, preferred_element_type=F32)
        where = pl.ds(pl.multiple_of(flip(frame, r) * fr, fr), fr)
        if k > 0:
            part = out_ref[0, :, where] + part
            sums = cols[r] + sums
        if k == npix - 1:
            part = part * state["row"] * (1.0 / sums)
        else:
            cols[r] = sums
        out_ref[0, :, where] = part

    def near(k):
        own(k)
        if k == npix - 1:
            state["row"] = state["count"] / state["sum"]
        for r in (0, 2, 4):
            tile(r, k)
        landed(1, k)
        tile(1, k)

    def relayed(k):
        for r in (3, 5):
            landed(r, k)
            tile(r, k)

    def far(k):
        tile(6, k)
        landed(7, k)
        tile(7, k)

    incoming = {}
    for k in range(1, npix):
        for piece in range(PIECES):
            part = rows(piece)
            incoming[k, piece] = send(packed.at[k - 1, part], grid.at[0, k, part], at_pix(k))
    stream = [(k, piece) for k in range(npix) for piece in range(PIECES)]
    total_pieces = len(stream)

    def begin(index):
        if stream[index] in incoming:
            incoming[stream[index]].wait_recv()
        spread(*stream[index])

    def finish(index):
        k, piece = stream[index]
        corner(k, piece)
        if piece == PIECES - 1:
            relayed(k)
            far(k)

    for index in range(LEAD):
        begin(index)
    for index, (k, piece) in enumerate(stream):
        if index + LEAD < total_pieces:
            begin(index + LEAD)
        relay(k, piece)
        if index >= LAG:
            finish(index - LAG)
        if piece == PIECES - 1:
            near(k)
    for index in range(total_pieces - LAG, total_pieces):
        finish(index)
    for copy in copies:
        copy.wait_send()


def fused(npix, frames, roi_ids, roi_order):
    fr, npx = frames.shape
    slot = SLOT
    count = (9 * npix - 1) * PIECES
    return pl.pallas_call(
        functools.partial(kernel, npix),
        out_shape=jax.ShapeDtypeStruct((1, fr, 8 * fr), F32),
        in_specs=[pl.BlockSpec(memory_space=pltpu.HBM)] * 3,
        out_specs=pl.BlockSpec(memory_space=pltpu.VMEM),
        scratch_shapes=[
            pltpu.SMEM((npix,), jnp.int32),
            pltpu.VMEM((1, npx), jnp.int32),
            pltpu.VMEM((fr, npx), F32),
            pltpu.VMEM((npix - 1, slot, fr), F32),
            pltpu.VMEM((8, npix, slot, fr), F32),
            pltpu.VMEM((npix, fr, 3 * slot), BF16),
            pltpu.VMEM((8, 1, fr), F32),
            pltpu.SemaphoreType.DMA((3,)),
            pltpu.SemaphoreType.DMA((count,)),
            pltpu.SemaphoreType.DMA((count,)),
        ],
        compiler_params=pltpu.CompilerParams(
            collective_id=0, has_side_effects=True, vmem_limit_bytes=40 * 1024 * 1024
        ),
    )(*(pltpu.with_memory_space_constraint(x, pltpu.HBM) for x in (roi_order, roi_ids.reshape(1, npx), frames)))


def shifted(value, axis, steps):
    count = lax.axis_size(axis)
    pairs = [(source, (source + steps) % count) for source in range(count)]
    return lax.ppermute(value, axis, pairs)


def per_device(frames, roi_ids, roi_order):
    fr_dev, pix_dev = frames.shape
    npix = lax.axis_size("pix")
    nframe = lax.axis_size("frame")
    rois = roi_order.shape[0]
    roi_dev = rois // npix
    slot = SLOT
    ids = roi_ids[:, 0]
    labels = jnp.arange(rois, dtype=jnp.int32)
    onehot = (ids[:, None] == labels[None, :]).astype(jnp.int32)
    rank = jnp.sum(onehot * (jnp.cumsum(onehot, axis=0) - 1), axis=1)
    holder = (roi_order[None, :] == labels[:, None]).astype(jnp.int32)
    position = jnp.sum(holder * labels[None, :], axis=1)
    target = jnp.sum(onehot * position[None, :], axis=1) * slot + rank
    buffer = jnp.zeros((rois * slot, fr_dev), jnp.float32).at[target].set(frames.T)
    buffer = buffer.reshape(npix, roi_dev, slot, fr_dev)
    local_counts = jnp.sum(onehot, axis=0)
    slot_counts = (
        jnp.sum(holder * local_counts[:, None], axis=0).astype(jnp.float32).reshape(npix, roi_dev)
    )
    own, arrived_counts = (
        lax.all_to_all(buffer, "pix", split_axis=0, concat_axis=0, tiled=True),
        lax.all_to_all(slot_counts, "pix", split_axis=0, concat_axis=0, tiled=True),
    )
    total = jnp.sum(arrived_counts, axis=0)
    own_sums = jnp.sum(own, axis=(0, 2))
    me = lax.axis_index("frame")
    width = fr_dev * nframe

    def make_tile(block):
        gram = jnp.einsum(
            "skpa,skpb->kab",
            own,
            block,
            precision=lax.Precision.HIGHEST,
            preferred_element_type=jnp.float32,
        )
        other = jnp.sum(block, axis=(0, 2))
        return total[:, None, None] * gram / (own_sums[:, :, None] * other[:, None, :])

    def place(result, block, start):
        tile = make_tile(block)
        return lax.dynamic_update_slice(result, tile, (jnp.int32(0), jnp.int32(0), start))

    result = jnp.zeros((roi_dev, fr_dev, width), jnp.float32)
    result = place(result, own, me * fr_dev)

    def turn(step, carry):
        moving, partial_out = carry
        moving = shifted(moving, "frame", 1)
        column = (me - step) % nframe
        return (moving, place(partial_out, moving, column * fr_dev))

    moving, result = lax.fori_loop(1, nframe, turn, (own, result))
    return result


def solution(mesh):
    npix, nframe = mesh.shape["pix"], mesh.shape["frame"]
    placed = (P("frame", "pix"), P("pix", None), P())

    def body(frames, roi_ids, roi_order):
        paired = nframe == 8 and npix & (npix - 1) == 0 and roi_order.shape[0] == npix
        if paired:
            return fused(npix, frames, roi_ids, roi_order)
        return per_device(frames, roi_ids, roi_order)

    return jax.shard_map(
        body, mesh=mesh, in_specs=placed, out_specs=P("pix", "frame", None), check_vma=False
    )
```
